128 devices in a mesh: dp: 8 (over y, core), head: 16 (over z, x).
Axes of the slice: x: 4, y: 4, z: 4, core: 2. Of those that a mesh axis runs over, the one named last changes fastest.
Arguments:
- hidden: bfloat16 [24576, 4096], P('dp'), may hold values from -6 to 6
- weight: bfloat16 [4096, 4096], P('head'), may hold values from -0.09375 to 0.09375
- block_ids: int32 [96, 8], P('dp'), may hold values from 0 to 31, all different within a row
- targets: int32 [24576, 8], P('dp'), may hold values from 0 to 4095
Outputs:
- grad_hidden: bfloat16 [24576, 4096], P('dp', 'head')
- grad_weight: bfloat16 [4096, 4096], P('head', 'dp')
The draws below stay inside these ranges and needn't reach their ends.
Inputs may be any that keep to these rules, and one draw needn't show every extreme that they name: `block_ids`: each row block lists 8 different label blocks; every label block is listed by some row block. `targets`: a row may repeat a label id.
All inputs are finite; a program needn't handle non-finite values.
Results may differ from the reference program's by a relative error of at most 0.014.
Values may be sent and summed in bfloat16 or wider, within the bound.
A program may use at most 128 MiB of HBM per device.

```python
import jax
import jax.numpy as jnp
from jax import lax

D = 4096
BLOCK = 128
ROWBLK = 256
SLOTS = 8
POS = 8
BPD = 2
NB = 32
LABELS = 4096
RBT = 96
ROWS = 24576
N_HEAD = 16


def touch_ends(values, rng, low, largest):
    longest = values.shape.index(max(values.shape))
    spots = []
    for shift in (0, 1):
        where = [jax.random.randint(jax.random.fold_in(rng, axis), (), 0, length) for axis, length in enumerate(values.shape)]
        where[longest] = (where[longest] + shift) % values.shape[longest]
        spots.append(tuple(where))
    return values.at[spots[0]].set(low).at[spots[1]].set(largest)


def block_scale(key, dims, shards, smallest, high):
    def one(dim, shards_of):
        draws = jax.random.uniform(jax.random.fold_in(jax.random.fold_in(key, 6), dim), (shards_of,), jnp.float32, smallest / len(shards), high / len(shards))
        return jnp.repeat(jnp.exp(draws), dims[dim] // shards_of).reshape((-1,) + (1,) * (len(dims) - dim - 1))

    factor_of = one(*shards[0])
    for cut in shards[1:]:
        factor_of = factor_of * one(*cut)
    return factor_of


def choose_distinct(own_key, rows, count, top, lift):
    ranking = jax.random.permutation(jax.random.fold_in(own_key, 1), count)
    favour = ranking
    for power in range(3):
        favour = favour * favour // count
    favour = favour * lift // count
    lots = jax.random.randint(jax.random.fold_in(own_key, 2), (rows, count), 0, 4096) + favour
    holders = jax.random.permutation(jax.random.fold_in(own_key, 3), rows)[jnp.arange(count) % rows]
    lots = jnp.where(jnp.arange(rows)[:, None] == holders[None, :], 1 << 14, lots)
    score = lots * count + jnp.arange(count)
    return lax.top_k(score.astype(jnp.int32), top)[1].astype(jnp.int32)


def bell_draw(key, shape, scale, most, cuts=(), held_as=jnp.bfloat16):
    level = block_scale(key, shape, cuts, -0.22, 0.18) if cuts else 1.0
    drawn = jax.random.normal(key, shape, jnp.float32) * scale * level
    return jnp.minimum(jnp.maximum(drawn, -most), most).astype(held_as)


def setup_inputs(seed: int = 0) -> dict:
    streams_of = jax.random.split(jax.random.key(seed), 5)
    return {
        "hidden": bell_draw(streams_of[0], (ROWS, D), 1.0, 6.0, ((0, 8),)),
        "weight": bell_draw(streams_of[1], (LABELS, D), D ** -0.5, 0.09375, ((0, 16),)),
        "block_ids": choose_distinct(streams_of[2], RBT, NB, SLOTS, 4096),
        "targets": touch_ends(jax.random.randint(streams_of[3], (ROWS, POS), 0, LABELS), jax.random.fold_in(streams_of[3], 1), 0, LABELS - 1).astype(jnp.int32),
    }


def reference(hidden, weight, block_ids, targets):
    blocks = weight.reshape(NB, BLOCK, D)
    hid3 = hidden.reshape(RBT, ROWBLK, D)
    tgt3 = targets.reshape(RBT, ROWBLK, POS)
    offsets = jnp.arange(BLOCK, dtype=jnp.int32)
    groups = jnp.arange(N_HEAD, dtype=jnp.int32)

    def step(carry, item):
        rows, ids, tgt = item
        chosen = blocks[ids]
        logits = jnp.dot(rows, chosen.reshape(SLOTS * BLOCK, D).T, preferred_element_type=jnp.float32)
        labels = (ids[:, None] * BLOCK + offsets[None, :]).reshape(-1)
        hits = jnp.any(tgt[:, :, None] == labels[None, None, :], axis=1)
        grads = (jax.nn.sigmoid(logits) - hits.astype(jnp.float32)).astype(jnp.bfloat16)
        grads3 = grads.reshape(ROWBLK, SLOTS, BLOCK).astype(jnp.float32)
        terms = jnp.einsum('rkj,kjd->krd', grads3, chosen.astype(jnp.float32))
        owner = ((ids // BPD)[:, None] == groups[None, :]).astype(jnp.float32)
        parts = jnp.einsum('ko,krd->ord', owner, terms, precision=lax.Precision.HIGHEST)
        rounded = lax.optimization_barrier(parts.astype(jnp.bfloat16))
        grad_rows = jnp.sum(rounded.astype(jnp.float32), axis=0).astype(jnp.bfloat16)
        contrib = jnp.einsum('rkj,rd->kjd', grads3, rows.astype(jnp.float32))
        carry = carry.at[ids].add(contrib)
        return carry, grad_rows

    start = jnp.zeros((NB, BLOCK, D), jnp.float32)
    total, grad_rows = lax.scan(step, start, (hid3, block_ids, tgt3))
    grad_hidden = grad_rows.reshape(ROWS, D)
    grad_weight = total.reshape(LABELS, D).astype(jnp.bfloat16)
    return grad_hidden, grad_weight
```

```python
import functools

import jax
import jax.numpy as jnp
from jax import lax
from jax.experimental import pallas as pl
from jax.experimental.pallas import tpu as pltpu
from jax.sharding import PartitionSpec as P

MESH = pl.DeviceIdType.MESH
BLOCK = 128
F32 = jnp.float32
BF16 = jnp.bfloat16


def kernel(ids_ref, tgt_ref, hid_hbm, w_hbm, gh_hbm, gw_hbm,
           hid, w, wq, g, gt, p, a1, b1, a2, b2, dl, dr, out,
           gwt, gwx, ga1, gb1, ga2, gb2, gdl, gdr, gwo,
           hid_sem, w_sem, out_sem, gwo_sem,
           wz_s, wz_r, wy_s, wy_r, wc_s, wc_r,
           own_s, own_r, fwd_s, fwd_r, hop_s, hop_r, dir_s, dir_r, two_s, two_r,
           gx_s, gx_r, gy_s, gy_r):
    rows = hid.shape[0]
    rb = 256
    half = rb // 2
    n = rows // rb
    dp = lax.axis_index("dp")
    head = lax.axis_index("head")
    y, core = dp // 2, dp % 2
    z, x = head // 4, head % 4

    def up(v, k):
        return lax.rem(v + k, 4)

    zR, zL, zO = up(z, 1), up(z, 3), up(z, 2)
    xR, xL, xO = up(x, 1), up(x, 3), up(x, 2)
    yR, yL, yO = up(y, 1), up(y, 3), up(y, 2)

    def at_z(zz):
        return (dp, zz * 4 + x)

    def at_x(xx):
        return (dp, z * 4 + xx)

    def at_y(yy):
        return (yy * 2 + core, head)

    sibling = (y * 2 + 1 - core, head)

    def remote(src, dst, ss, rs, dev):
        return pltpu.make_async_remote_copy(
            src_ref=src, dst_ref=dst, send_sem=ss, recv_sem=rs, device_id=dev, device_id_type=MESH)

    def chunk(c):
        return pl.ds(pl.multiple_of(c * rb, rb), rb)

    def half_a(c):
        return pl.ds(pl.multiple_of(c * rb, rb), half)

    def half_b(c):
        return pl.ds(pl.multiple_of(c * rb + half, half), half)

    def load_hid(c):
        return pltpu.make_async_copy(hid_hbm.at[chunk(c)], hid.at[chunk(c)], hid_sem.at[c])

    load_w = pltpu.make_async_copy(w_hbm, w, w_sem.at[0])
    load_wq = pltpu.make_async_copy(
        w_hbm.at[:, pl.ds(pl.multiple_of(z * 1024, 1024), 1024)], wq.at[0], w_sem.at[1])

    load_w.start()
    load_hid(0).start()
    load_hid(1).start()
    load_wq.start()

    @pl.loop(2, n)
    def _(c):
        load_hid(c).start()

    barrier = pltpu.get_barrier_semaphore()
    for dev in (at_z(zR), at_z(zL), at_z(zO), at_x(xR), at_x(xL), at_y(yR), at_y(yL), at_y(yO), sibling):
        pl.semaphore_signal(barrier, inc=1, device_id=dev, device_id_type=MESH)
    pl.semaphore_wait(barrier, 9)

    piece = 32
    mine = pl.ds(pl.multiple_of(dp * piece, piece), piece)

    def wz(k):
        to = (zR, zL, zO)[k]
        return remote(w_hbm.at[mine, pl.ds(pl.multiple_of(to * 1024, 1024), 1024)],
                      wq.at[k + 1, mine], wz_s.at[k], wz_r.at[k], at_z(to))

    def wy(k):
        to = (yR, yL, yO)[k]
        return remote(wq.at[pl.ds(1, 3), mine], wq.at[pl.ds(1, 3), mine], wy_s.at[k], wy_r.at[k], at_y(to))

    def wc(k):
        frm = ((y, yL, yR, yO)[k]) * 2 + core
        part = pl.ds(pl.multiple_of(frm * piece, piece), piece)
        return remote(wq.at[pl.ds(1, 3), part], wq.at[pl.ds(1, 3), part], wc_s.at[k], wc_r.at[k], sibling)

    for k in range(3):
        wz(k).start()

    def own_R(c):
        return remote(g.at[0, chunk(c)], g.at[1, chunk(c)], own_s.at[0, c], own_r.at[0, c], at_z(zR))

    def own_L(c):
        return remote(g.at[0, chunk(c)], g.at[2, chunk(c)], own_s.at[1, c], own_r.at[1, c], at_z(zL))

    def fwd_R(c):
        return remote(g.at[1, half_a(c)], g.at[3, half_a(c)], fwd_s.at[0, c], fwd_r.at[0, c], at_z(zR))

    def fwd_L(c):
        return remote(g.at[2, half_b(c)], g.at[3, half_b(c)], fwd_s.at[1, c], fwd_r.at[1, c], at_z(zL))

    def hop_R(c):
        return remote(p.at[xO, half_a(c)], a1.at[c], hop_s.at[0, c], hop_r.at[0, c], at_x(xR))

    def hop_L(c):
        return remote(p.at[xO, half_b(c)], b1.at[c], hop_s.at[1, c], hop_r.at[1, c], at_x(xL))

    def dir_R(c):
        return remote(p.at[xR, half_b(c)], dl.at[c], dir_s.at[0, c], dir_r.at[0, c], at_x(xR))

    def dir_L(c):
        return remote(p.at[xL, half_a(c)], dr.at[c], dir_s.at[1, c], dir_r.at[1, c], at_x(xL))

    def two_R(c):
        return remote(a1.at[c], a2.at[c], two_s.at[0, c], two_r.at[0, c], at_x(xR))

    def two_L(c):
        return remote(b1.at[c], b2.at[c], two_s.at[1, c], two_r.at[1, c], at_x(xL))

    def store_out(c):
        return pltpu.make_async_copy(out.at[chunk(c)], gh_hbm.at[chunk(c)], out_sem.at[c])

    first = head * 2
    labels = first * BLOCK + lax.broadcasted_iota(jnp.int32, (256, rb), 0)

    def signal(c):
        load_hid(c).wait()
        t = lax.dot_general(w[...], hid[chunk(c), :], (((1,), (1,)), ((), ())), preferred_element_type=F32)
        lo = jnp.int32(0)
        hi = jnp.int32(0)
        for k in range(ids_ref.shape[0]):
            ident = ids_ref[k, c]
            lo = lo + (ident == first).astype(jnp.int32)
            hi = hi + (ident == first + 1).astype(jnp.int32)
        tg = tgt_ref[:, chunk(c)]
        hits = labels == tg[0:1, :]
        for k in range(1, tgt_ref.shape[0]):
            hits = hits | (labels == tg[k:k + 1, :])
        s = jax.nn.sigmoid(t) - hits.astype(F32)
        block = lax.broadcasted_iota(jnp.int32, (256, rb), 0) // BLOCK
        on = jnp.where(block == 0, lo, hi) > 0
        s = jnp.where(on, s, 0.0)
        gt[:, chunk(c)] = s.astype(BF16)
        g[0, chunk(c), :] = s.T.astype(BF16)

    def gw_tile(j):
        cols = pl.ds(pl.multiple_of(j * 512, 512), 512)
        t = jnp.dot(gt[...], hid[:, cols], preferred_element_type=F32)
        gwt[j] = t.astype(BF16)

    def gx(k):
        return remote(gwt.at[2 * k + 1 - core], gwx.at[k], gx_s.at[k], gx_r.at[k], sibling)

    A, B = pl.ds(0, 128), pl.ds(128, 128)

    def gy(k):
        src, dst, to = (
            (gwx.at[yO, A], ga1, yR), (gwx.at[yO, B], gb1, yL),
            (gwx.at[yR, B], gdl, yR), (gwx.at[yL, A], gdr, yL),
            (ga1, ga2, yR), (gb1, gb2, yL))[k]
        return remote(src, dst, gy_s.at[k], gy_r.at[k], at_y(to))

    store_gw = pltpu.make_async_copy(gwo, gw_hbm, gwo_sem.at[0])

    load_w.wait()
    signal(0)
    load_wq.wait()
    for k in range(3):
        wz(k).wait_recv()
    for k in range(3):
        wy(k).start()
    wc(0).start()

    @pl.loop(0, n + 4)
    def _(s):
        @pl.when((s >= 1) & (s < n + 1))
        def _():
            own_R(s - 1).wait_recv()
            own_L(s - 1).wait_recv()
            fwd_R(s - 1).start()
            fwd_L(s - 1).start()

        @pl.when(s < n)
        def _():
            own_R(s).start()
            own_L(s).start()

        @pl.when(s == 1)
        def _():
            for k in range(3):
                wy(k).wait_recv()
            for k in range(1, 4):
                wc(k).start()

        @pl.when(s == 2)
        def _():
            for k in range(4):
                wc(k).wait_recv()

        @pl.when((s >= 2) & (s < n + 2))
        def _():
            c = s - 2
            fwd_R(c).wait_recv()
            fwd_L(c).wait_recv()
            lhs = jnp.concatenate([g[k, chunk(c), :] for k in range(4)], axis=1)
            rhs = wq[...].reshape(1024, 1024)
            part = jnp.dot(lhs, rhs, preferred_element_type=F32).astype(BF16)
            for k in range(4):
                p[k, chunk(c), :] = part[:, k * 256:(k + 1) * 256]
            hop_R(c).start()
            hop_L(c).start()
            dir_R(c).start()
            dir_L(c).start()

        @pl.when((s >= 3) & (s < n + 3))
        def _():
            c = s - 3
            hop_R(c).wait_recv()
            a1[c] = (a1[c].astype(F32) + p[xR, half_a(c), :].astype(F32)).astype(BF16)
            two_R(c).start()
            hop_L(c).wait_recv()
            b1[c] = (b1[c].astype(F32) + p[xL, half_b(c), :].astype(F32)).astype(BF16)
            two_L(c).start()

        @pl.when(s >= 4)
        def _():
            c = s - 4
            dir_L(c).wait_recv()
            two_R(c).wait_recv()
            out[half_a(c), :] = (p[x, half_a(c), :].astype(F32) + a2[c].astype(F32) + dr[c].astype(F32)).astype(BF16)
            dir_R(c).wait_recv()
            two_L(c).wait_recv()
            out[half_b(c), :] = (p[x, half_b(c), :].astype(F32) + b2[c].astype(F32) + dl[c].astype(F32)).astype(BF16)
            store_out(c).start()
            for copy in (own_R, own_L, fwd_R, fwd_L, hop_R, hop_L, dir_R, dir_L, two_R, two_L):
                copy(c).wait_send()

        @pl.when(s < 6)
        def _():
            signal(2 * s + 1)

        @pl.when(s < 5)
        def _():
            signal(2 * s + 2)

        @pl.when((s >= 6) & (s < 10))
        def _():
            for k in range(2):
                i = 2 * (s - 6) + k
                gw_tile(2 * lax.rem(i, 4) + jnp.where(i < 4, 1 - core, core))

        @pl.when((s == 6) | (s == 7))
        def _():
            gx(2 * (s - 6)).start()
            gx(2 * (s - 6) + 1).start()

        @pl.when(s == 10)
        def _():
            for k in range(4):
                gx(k).wait_recv()
                gwx[k] = (gwx[k].astype(F32) + gwt[2 * k + core].astype(F32)).astype(BF16)
            for k in range(4):
                gy(k).start()

        @pl.when(s == 11)
        def _():
            gy(0).wait_recv()
            ga1[...] = (ga1[...].astype(F32) + gwx[yR, A, :].astype(F32)).astype(BF16)
            gy(4).start()
            gy(1).wait_recv()
            gb1[...] = (gb1[...].astype(F32) + gwx[yL, B, :].astype(F32)).astype(BF16)
            gy(5).start()

        @pl.when(s == 13)
        def _():
            gy(3).wait_recv()
            gy(4).wait_recv()
            gwo[A, :] = (gwx[y, A, :].astype(F32) + ga2[...].astype(F32) + gdr[...].astype(F32)).astype(BF16)
            gy(2).wait_recv()
            gy(5).wait_recv()
            gwo[B, :] = (gwx[y, B, :].astype(F32) + gb2[...].astype(F32) + gdl[...].astype(F32)).astype(BF16)
            store_gw.start()

    for k in range(3):
        wz(k).wait_send()
        wy(k).wait_send()
    for k in range(4):
        wc(k).wait_send()
        gx(k).wait_send()
    for k in range(6):
        gy(k).wait_send()

    @pl.loop(0, n)
    def _(c):
        store_out(c).wait()
    store_gw.wait()


def local(hidden, weight, block_ids, targets):
    rows, width = hidden.shape
    owned = weight.shape[0]
    n = rows // 256
    dma = pltpu.SemaphoreType.DMA
    v = lambda *shape: pltpu.VMEM(shape, BF16)
    scratch = [
        v(rows, width), v(owned, width), v(4, owned, 1024), v(4, rows, owned), v(owned, rows), v(4, rows, 256),
        v(n, 128, 256), v(n, 128, 256), v(n, 128, 256), v(n, 128, 256), v(n, 128, 256), v(n, 128, 256),
        v(rows, 256),
        v(8, owned, 512), v(4, owned, 512),
        v(128, 512), v(128, 512), v(128, 512), v(128, 512), v(128, 512), v(128, 512), v(owned, 512),
        dma((n,)), dma((2,)), dma((n,)), dma((1,)),
        dma((3,)), dma((3,)), dma((3,)), dma((3,)), dma((4,)), dma((4,)),
    ] + [dma((2, n))] * 10 + [dma((4,)), dma((4,)), dma((6,)), dma((6,))]
    anywhere = pl.BlockSpec(memory_space=pl.ANY)
    return pl.pallas_call(
        kernel,
        out_shape=(jax.ShapeDtypeStruct((rows, 256), BF16), jax.ShapeDtypeStruct((owned, 512), BF16)),
        in_specs=[pl.BlockSpec(memory_space=pltpu.SMEM), pl.BlockSpec(memory_space=pltpu.VMEM), anywhere, anywhere],
        out_specs=(anywhere, anywhere),
        scratch_shapes=scratch,
        compiler_params=pltpu.CompilerParams(
            collective_id=0, has_side_effects=True, vmem_limit_bytes=60 * 1024 * 1024),
        cost_estimate=pl.CostEstimate(flops=3 * 2 * rows * owned * width, bytes_accessed=2 * rows * width, transcendentals=rows * owned),
    )(block_ids.T, targets.T, hidden, weight)


def solution(mesh):
    return jax.shard_map(
        local,
        mesh=mesh,
        in_specs=(P("dp", None), P("head", None), P("dp", None), P("dp", None)),
        out_specs=(P("dp", "head"), P("head", "dp")),
        check_vma=False,
    )
```

```python
import jax
import jax.numpy as jnp
from jax import lax
from jax.experimental import pallas as pl
from jax.experimental.pallas import tpu as pltpu
from jax.sharding import PartitionSpec as P

MESH = pl.DeviceIdType.MESH
BLOCK = 128
F32 = jnp.float32
BF16 = jnp.bfloat16
RL = 256
RB = 128


def kernel(ids_ref, tgt_ref, hid_hbm, w_hbm, gh_hbm, gw_hbm,
           hid, w, wq, g, gt, p, a1, b1, a2, b2, dl, dr, out,
           gwt, gwx, ga1, gb1, ga2, gb2, gdl, gdr, gwo,
           hid_sem, w_sem, out_sem, gwo_sem,
           wz_s, wz_r, wx_s, wx_r, wy_s, wy_r, wc_s, wc_r,
           own_s, own_r, fwd_s, fwd_r, hop_s, hop_r, dir_s, dir_r, two_s, two_r,
           gx_s, gx_r, gy_s, gy_r):
    rows = hid.shape[0]
    half = RB // 2
    nb = rows // RL
    nc = rows // RB
    dp = lax.axis_index("dp")
    head = lax.axis_index("head")
    y, core = dp // 2, dp % 2
    z, x = head // 4, head % 4

    def ring(v):
        return lax.rem(v + 1, 4), lax.rem(v + 3, 4), lax.rem(v + 2, 4)

    zs, xs, ys = ring(z), ring(x), ring(y)
    to_z = [(dp, v * 4 + x) for v in zs]
    to_x = [(dp, z * 4 + v) for v in xs]
    to_y = [(v * 2 + core, head) for v in ys]
    gather_to = (to_z, to_x)
    reduce_to = (to_x, to_z)
    reduce_at = (xs, zs)
    reduce_me = (x, z)
    sibling = (y * 2 + 1 - core, head)

    def remote(src, dst, ss, rs, dev):
        return pltpu.make_async_remote_copy(
            src_ref=src, dst_ref=dst, send_sem=ss, recv_sem=rs, device_id=dev, device_id_type=MESH)

    def span(start, size):
        return pl.ds(pl.multiple_of(start, size), size)

    def block(b):
        return span(b * RL, RL)

    def low(b):
        return span(b * RL, RL // 2)

    def high(b):
        return span(b * RL + RL // 2, RL // 2)

    def half_a(c):
        return span(c * RB, half)

    def half_b(c):
        return span(c * RB + half, half)

    def load_hid(b):
        return pltpu.make_async_copy(hid_hbm.at[block(b)], hid.at[block(b)], hid_sem.at[b])

    load_w = pltpu.make_async_copy(w_hbm, w, w_sem.at[0])
    load_wz = pltpu.make_async_copy(w_hbm.at[:, span(z * 1024, 1024)], wq.at[0, 0], w_sem.at[1])

    def load_wx(k):
        return pltpu.make_async_copy(
            w_hbm.at[:, span((k * 4 + x) * 256, 256)], wq.at[1, 0, :, pl.ds(k * 256, 256)], w_sem.at[2 + k])

    load_w.start()
    load_hid(0).start()
    load_hid(nb // 2).start()

    @pl.loop(1, nb // 2)
    def _(b):
        load_hid(b).start()
        load_hid(b + nb // 2).start()

    load_wz.start()
    for k in range(4):
        load_wx(k).start()

    barrier = pltpu.get_barrier_semaphore()
    peers = to_z + to_x + to_y + [sibling]
    for dev in peers:
        pl.semaphore_signal(barrier, inc=1, device_id=dev, device_id_type=MESH)
    pl.semaphore_wait(barrier, len(peers))

    piece = w.shape[0] // 8
    mine = span(dp * piece, piece)

    def wz(k):
        return remote(w_hbm.at[mine, span(zs[k] * 1024, 1024)], wq.at[0, k + 1, mine],
                      wz_s.at[k], wz_r.at[k], to_z[k])

    def wx(k, j):
        return remote(w_hbm.at[mine, span((j * 4 + xs[k]) * 256, 256)], wq.at[1, k + 1, mine, pl.ds(j * 256, 256)],
                      wx_s.at[k, j], wx_r.at[k, j], to_x[k])

    def wy(o, k):
        part = wq.at[o, pl.ds(1, 3), mine]
        return remote(part, part, wy_s.at[o, k], wy_r.at[o, k], to_y[k])

    def wc(o, k):
        frm = (y, ys[1], ys[0], ys[2])[k] * 2 + core
        part = wq.at[o, pl.ds(1, 3), span(frm * piece, piece)]
        return remote(part, part, wc_s.at[o, k], wc_r.at[o, k], sibling)

    for k in range(3):
        wz(k).start()
        for j in range(4):
            wx(k, j).start()

    def own(o, k, b):
        return remote(g.at[0, block(b)], g.at[k + 1, block(b)], own_s.at[k, b], own_r.at[k, b], gather_to[o][k])

    def fwd(o, k, b):
        part = (low, high)[k](b)
        return remote(g.at[k + 1, part], g.at[3, part], fwd_s.at[k, b], fwd_r.at[k, b], gather_to[o][k])

    def hop(o, k, c):
        part, dst = ((half_a(c), a1), (half_b(c), b1))[k]
        return remote(p.at[reduce_at[o][2], part], dst.at[c], hop_s.at[k, c], hop_r.at[k, c], reduce_to[o][k])

    def direct(o, k, c):
        part, dst = ((half_b(c), dl), (half_a(c), dr))[k]
        return remote(p.at[reduce_at[o][k], part], dst.at[c], dir_s.at[k, c], dir_r.at[k, c], reduce_to[o][k])

    def two(o, k, c):
        src, dst = ((a1, a2), (b1, b2))[k]
        return remote(src.at[c], dst.at[c], two_s.at[k, c], two_r.at[k, c], reduce_to[o][k])

    def store_out(c):
        return pltpu.make_async_copy(out.at[span(c * RB, RB)], gh_hbm.at[span(c * RB, RB)], out_sem.at[c])

    first = head * 2
    labels = first * BLOCK + lax.broadcasted_iota(jnp.int32, (2 * BLOCK, RL), 0)
    upper = lax.broadcasted_iota(jnp.int32, (2 * BLOCK, RL), 0) >= BLOCK

    def signal(b):
        load_hid(b).wait()
        t = lax.dot_general(w[...], hid[block(b), :], (((1,), (1,)), ((), ())), preferred_element_type=F32)
        lo = jnp.int32(0)
        hi = jnp.int32(0)
        for k in range(ids_ref.shape[0]):
            ident = ids_ref[k, b]
            lo = lo + (ident == first).astype(jnp.int32)
            hi = hi + (ident == first + 1).astype(jnp.int32)
        tg = tgt_ref[:, block(b)]
        hits = labels == tg[0:1, :]
        for k in range(1, tgt_ref.shape[0]):
            hits = hits | (labels == tg[k:k + 1, :])
        s = jax.nn.sigmoid(t) - hits.astype(F32)
        s = jnp.where(jnp.where(upper, hi, lo) > 0, s, 0.0)
        gt[:, block(b)] = s.astype(BF16)
        g[0, block(b), :] = s.T.astype(BF16)

    def gw_tile(j):
        t = jnp.dot(gt[...], hid[:, span(j * 512, 512)], preferred_element_type=F32)
        gwt[j] = t.astype(BF16)

    def gx(k):
        return remote(gwt.at[2 * k + 1 - core], gwx.at[k], gx_s.at[k], gx_r.at[k], sibling)

    A, B = pl.ds(0, 128), pl.ds(128, 128)

    def gy(k):
        src, dst, to = (
            (gwx.at[ys[2], A], ga1, 0), (gwx.at[ys[2], B], gb1, 1),
            (gwx.at[ys[0], B], gdl, 0), (gwx.at[ys[1], A], gdr, 1),
            (ga1, ga2, 0), (gb1, gb2, 1))[k]
        return remote(src, dst, gy_s.at[k], gy_r.at[k], to_y[to])

    store_gw = pltpu.make_async_copy(gwo, gw_hbm, gwo_sem.at[0])

    def add(*parts):
        total = parts[0].astype(F32)
        for part in parts[1:]:
            total = total + part.astype(F32)
        return total.astype(BF16)

    load_w.wait()

    nh = nb // 2
    LA = 2

    @pl.loop(0, nh + 4)
    def _(s):
        for o in range(2):
            @pl.when(s < nh)
            def _():
                b = s + o * nh
                signal(b)
                for k in range(2):
                    own(o, k, b).start()

            @pl.when((s >= LA) & (s < nh + LA))
            def _():
                b = s - LA + o * nh
                for k in range(2):
                    own(o, k, b).wait_recv()
                    fwd(o, k, b).start()

        @pl.when(s == 1)
        def _():
            load_wz.wait()
            for k in range(4):
                load_wx(k).wait()
            for k in range(3):
                wz(k).wait_recv()
                for j in range(4):
                    wx(k, j).wait_recv()
            for o in range(2):
                for k in range(3):
                    wy(o, k).start()
                wc(o, 0).start()

        @pl.when(s == 7)
        def _():
            for o in range(2):
                for k in range(3):
                    wy(o, k).wait_recv()
                    wc(o, k + 1).start()

        @pl.when(s >= nh)
        def _():
            for k in range(2):
                i = 2 * (s - nh) + k
                gw_tile(2 * lax.rem(i, 4) + jnp.where(i < 4, 1 - core, core))

        @pl.when((s >= nh) & (s < nh + 2))
        def _():
            for k in range(2):
                gx(2 * (s - nh) + k).start()

    for o in range(2):
        for k in range(4):
            wc(o, k).wait_recv()

    mh = nc // 2
    LD = 2
    LE = 4

    @pl.loop(0, mh + LE)
    def _(s):
        @pl.when(s < mh)
        def _():
            @pl.when(s % 2 == 0)
            def _():
                for o in range(2):
                    for k in range(2):
                        fwd(o, k, s // 2 + o * nh).wait_recv()

            for o in range(2):
                c = s + o * mh
                lhs = jnp.concatenate([g[k, span(c * RB, RB), :] for k in range(4)], axis=1)
                part = jnp.dot(lhs, wq[o].reshape(1024, 1024), preferred_element_type=F32).astype(BF16)
                for k in range(4):
                    p[k, span(c * RB, RB), :] = part[:, k * 256:(k + 1) * 256]
                for k in range(2):
                    hop(o, k, c).start()
                for k in range(2):
                    direct(o, k, c).start()

        @pl.when((s >= LD) & (s < mh + LD))
        def _():
            for o in range(2):
                c = s - LD + o * mh
                right, left, _ = reduce_at[o]
                hop(o, 0, c).wait_recv()
                a1[c] = add(a1[c], p[right, half_a(c), :])
                two(o, 0, c).start()
                hop(o, 1, c).wait_recv()
                b1[c] = add(b1[c], p[left, half_b(c), :])
                two(o, 1, c).start()

        @pl.when(s >= LE)
        def _():
            for o in range(2):
                c = s - LE + o * mh
                me = reduce_me[o]
                direct(o, 1, c).wait_recv()
                two(o, 0, c).wait_recv()
                out[half_a(c), :] = add(p[me, half_a(c), :], a2[c], dr[c])
                direct(o, 0, c).wait_recv()
                two(o, 1, c).wait_recv()
                out[half_b(c), :] = add(p[me, half_b(c), :], b2[c], dl[c])
                store_out(c).start()

        @pl.when(s == 0)
        def _():
            for k in range(4):
                gx(k).wait_recv()
                gwx[k] = add(gwx[k], gwt[2 * k + core])
            for k in range(4):
                gy(k).start()

        @pl.when(s == 4)
        def _():
            gy(0).wait_recv()
            ga1[...] = add(ga1[...], gwx[ys[0], A, :])
            gy(4).start()
            gy(1).wait_recv()
            gb1[...] = add(gb1[...], gwx[ys[1], B, :])
            gy(5).start()

        @pl.when(s == 8)
        def _():
            gy(3).wait_recv()
            gy(4).wait_recv()
            gwo[A, :] = add(gwx[y, A, :], ga2[...], gdr[...])
            gy(2).wait_recv()
            gy(5).wait_recv()
            gwo[B, :] = add(gwx[y, B, :], gb2[...], gdl[...])
            store_gw.start()

    for k in range(3):
        wz(k).wait_send()
        for j in range(4):
            wx(k, j).wait_send()
        for o in range(2):
            wy(o, k).wait_send()
    for k in range(4):
        gx(k).wait_send()
        for o in range(2):
            wc(o, k).wait_send()
    for k in range(6):
        gy(k).wait_send()

    @pl.loop(0, nh)
    def _(s):
        for o in range(2):
            for k in range(2):
                own(o, k, s + o * nh).wait_send()
                fwd(o, k, s + o * nh).wait_send()

    @pl.loop(0, mh)
    def _(s):
        for o in range(2):
            c = s + o * mh
            for k in range(2):
                hop(o, k, c).wait_send()
                direct(o, k, c).wait_send()
                two(o, k, c).wait_send()
            store_out(c).wait()

    store_gw.wait()


def local(hidden, weight, block_ids, targets):
    rows, width = hidden.shape
    owned = weight.shape[0]
    nb, nc = rows // RL, rows // RB
    dma = pltpu.SemaphoreType.DMA
    v = lambda *shape: pltpu.VMEM(shape, BF16)
    scratch = [
        v(rows, width), v(owned, width), v(2, 4, owned, 1024), v(4, rows, owned), v(owned, rows), v(4, rows, 256),
    ] + [v(nc, RB // 2, 256)] * 6 + [
        v(rows, 256), v(8, owned, 512), v(4, owned, 512),
    ] + [v(128, 512)] * 6 + [
        v(owned, 512),
        dma((nb,)), dma((6,)), dma((nc,)), dma((1,)),
        dma((3,)), dma((3,)), dma((3, 4)), dma((3, 4)), dma((2, 3)), dma((2, 3)), dma((2, 4)), dma((2, 4)),
    ] + [dma((2, nb))] * 4 + [dma((2, nc))] * 6 + [dma((4,)), dma((4,)), dma((6,)), dma((6,))]
    anywhere = pl.BlockSpec(memory_space=pl.ANY)
    return pl.pallas_call(
        kernel,
        out_shape=(jax.ShapeDtypeStruct((rows, 256), BF16), jax.ShapeDtypeStruct((owned, 512), BF16)),
        in_specs=[pl.BlockSpec(memory_space=pltpu.SMEM), pl.BlockSpec(memory_space=pltpu.VMEM), anywhere, anywhere],
        out_specs=(anywhere, anywhere),
        scratch_shapes=scratch,
        compiler_params=pltpu.CompilerParams(
            collective_id=0, has_side_effects=True, vmem_limit_bytes=60 * 1024 * 1024),
        cost_estimate=pl.CostEstimate(
            flops=6 * rows * owned * width, bytes_accessed=2 * rows * width, transcendentals=rows * owned),
    )(block_ids.T, targets.T, hidden, weight)


def solution(mesh):
    return jax.shard_map(
        local,
        mesh=mesh,
        in_specs=(P("dp", None), P("head", None), P("dp", None), P("dp", None)),
        out_specs=(P("dp", "head"), P("head", "dp")),
        check_vma=False,
    )
```

```python
import jax
import jax.numpy as jnp
from jax import lax
from jax.experimental import pallas as pl
from jax.experimental.pallas import tpu as pltpu
from jax.sharding import PartitionSpec as P

MESH = pl.DeviceIdType.MESH
BLOCK = 128
F32 = jnp.float32
BF16 = jnp.bfloat16
RL = 256
RB = 256


def kernel(ids_ref, tgt_ref, hid_hbm, w_hbm, out, gwo,
           hid, w, wq, g, gt, p, a1, b1, a2, b2, dl, dr,
           gwt, gwx, ga1, gb1, ga2, gb2, gdl, gdr,
           hid_sem, w_sem,
           wz_s, wz_r, wx_s, wx_r, wy_s, wy_r, wc_s, wc_r,
           own_s, own_r, fwd_s, fwd_r, hop_s, hop_r, dir_s, dir_r, two_s, two_r,
           gx_s, gx_r, gy_s, gy_r):
    rows = hid.shape[0]
    half = RB // 2
    nb = rows // RL
    nc = rows // RB
    dp = lax.axis_index("dp")
    head = lax.axis_index("head")
    y, core = dp // 2, dp % 2
    z, x = head // 4, head % 4

    def ring(v):
        return lax.rem(v + 1, 4), lax.rem(v + 3, 4), lax.rem(v + 2, 4)

    zs, xs, ys = ring(z), ring(x), ring(y)
    to_z = [(dp, v * 4 + x) for v in zs]
    to_x = [(dp, z * 4 + v) for v in xs]
    to_y = [(v * 2 + core, head) for v in ys]
    gather_to = (to_z, to_x)
    reduce_to = (to_x, to_z)
    reduce_at = (xs, zs)
    reduce_me = (x, z)
    sibling = (y * 2 + 1 - core, head)

    def remote(src, dst, ss, rs, dev):
        return pltpu.make_async_remote_copy(
            src_ref=src, dst_ref=dst, send_sem=ss, recv_sem=rs, device_id=dev, device_id_type=MESH)

    def span(start, size):
        return pl.ds(pl.multiple_of(start, size), size)

    def block(b):
        return span(b * RL, RL)

    def low(b):
        return span(b * RL, RL // 2)

    def high(b):
        return span(b * RL + RL // 2, RL // 2)

    def half_a(c):
        return span(c * RB, half)

    def half_b(c):
        return span(c * RB + half, half)

    def load_hid(b):
        return pltpu.make_async_copy(hid_hbm.at[block(b)], hid.at[block(b)], hid_sem.at[b])

    load_w = pltpu.make_async_copy(w_hbm, w, w_sem.at[0])
    load_wz = pltpu.make_async_copy(w_hbm.at[:, span(z * 1024, 1024)], wq.at[0, 0], w_sem.at[1])

    def load_wx(k):
        return pltpu.make_async_copy(
            w_hbm.at[:, span((k * 4 + x) * 256, 256)], wq.at[1, 0, :, pl.ds(k * 256, 256)], w_sem.at[2 + k])

    load_w.start()
    load_hid(0).start()
    load_hid(nb // 2).start()

    load_wz.start()
    for k in range(4):
        load_wx(k).start()

    barrier = pltpu.get_barrier_semaphore()
    peers = to_z + to_x + to_y + [sibling]
    for dev in peers:
        pl.semaphore_signal(barrier, inc=1, device_id=dev, device_id_type=MESH)
    pl.semaphore_wait(barrier, len(peers))

    piece = w.shape[0] // 8
    mine = span(dp * piece, piece)

    def wz(k):
        return remote(w_hbm.at[mine, span(zs[k] * 1024, 1024)], wq.at[0, k + 1, mine],
                      wz_s.at[k], wz_r.at[k], to_z[k])

    def wx(k, j):
        return remote(w_hbm.at[mine, span((j * 4 + xs[k]) * 256, 256)], wq.at[1, k + 1, mine, pl.ds(j * 256, 256)],
                      wx_s.at[k, j], wx_r.at[k, j], to_x[k])

    def wy(o, k):
        part = wq.at[o, pl.ds(1, 3), mine]
        return remote(part, part, wy_s.at[o, k], wy_r.at[o, k], to_y[k])

    def wc(o, k):
        frm = (y, ys[1], ys[0], ys[2])[k] * 2 + core
        part = wq.at[o, pl.ds(1, 3), span(frm * piece, piece)]
        return remote(part, part, wc_s.at[o, k], wc_r.at[o, k], sibling)

    for k in range(3):
        wz(k).start()
        for j in range(4):
            wx(k, j).start()

    def own(o, k, b):
        return remote(g.at[0, block(b)], g.at[k + 1, block(b)], own_s.at[k, b], own_r.at[k, b], gather_to[o][k])

    def fwd(o, k, b):
        part = (low, high)[k](b)
        return remote(g.at[k + 1, part], g.at[3, part], fwd_s.at[k, b], fwd_r.at[k, b], gather_to[o][k])

    def hop(o, k, c):
        part, dst = ((half_a(c), a1), (half_b(c), b1))[k]
        return remote(p.at[reduce_at[o][2], part], dst.at[c], hop_s.at[k, c], hop_r.at[k, c], reduce_to[o][k])

    def direct(o, k, c):
        part, dst = ((half_b(c), dl), (half_a(c), dr))[k]
        return remote(p.at[reduce_at[o][k], part], dst.at[c], dir_s.at[k, c], dir_r.at[k, c], reduce_to[o][k])

    def two(o, k, c):
        src, dst = ((a1, a2), (b1, b2))[k]
        return remote(src.at[c], dst.at[c], two_s.at[k, c], two_r.at[k, c], reduce_to[o][k])

    first = head * 2
    labels = first * BLOCK + lax.broadcasted_iota(jnp.int32, (2 * BLOCK, RL), 0)
    upper = lax.broadcasted_iota(jnp.int32, (2 * BLOCK, RL), 0) >= BLOCK

    def signal(b):
        load_hid(b).wait()
        t = lax.dot_general(w[...], hid[block(b), :], (((1,), (1,)), ((), ())), preferred_element_type=F32)
        lo = jnp.int32(0)
        hi = jnp.int32(0)
        for k in range(ids_ref.shape[0]):
            ident = ids_ref[k, b]
            lo = lo + (ident == first).astype(jnp.int32)
            hi = hi + (ident == first + 1).astype(jnp.int32)
        tg = tgt_ref[:, block(b)]
        hits = labels == tg[0:1, :]
        for k in range(1, tgt_ref.shape[0]):
            hits = hits | (labels == tg[k:k + 1, :])
        s = jax.nn.sigmoid(t) - hits.astype(F32)
        s = jnp.where(jnp.where(upper, hi, lo) > 0, s, 0.0)
        gt[:, block(b)] = s.astype(BF16)
        g[0, block(b), :] = s.T.astype(BF16)

    def gw_tile(j):
        t = jnp.dot(gt[...], hid[:, span(j * 512, 512)], preferred_element_type=F32)
        gwt[j] = t.astype(BF16)

    def gx(k):
        return remote(gwt.at[2 * k + 1 - core], gwx.at[k], gx_s.at[k], gx_r.at[k], sibling)

    A, B = pl.ds(0, 128), pl.ds(128, 128)

    def gy(k):
        src, dst, to = (
            (gwx.at[ys[2], A], ga1, 0), (gwx.at[ys[2], B], gb1, 1),
            (gwx.at[ys[0], B], gdl, 0), (gwx.at[ys[1], A], gdr, 1),
            (ga1, ga2, 0), (gb1, gb2, 1))[k]
        return remote(src, dst, gy_s.at[k], gy_r.at[k], to_y[to])

    def add(*parts):
        total = parts[0].astype(F32)
        for part in parts[1:]:
            total = total + part.astype(F32)
        return total.astype(BF16)

    load_w.wait()

    nh = nb // 2
    for o in range(2):
        load_hid(o * nh + 1).start()

    LA = 3

    @pl.loop(0, nh + 4)
    def _(s):
        for o in range(2):
            @pl.when(s < nh)
            def _():
                b = s + o * nh

                @pl.when(s < nh - 2)
                def _():
                    load_hid(b + 2).start()

                signal(b)
                for k in range(2):
                    own(o, k, b).start()

            @pl.when((s >= LA) & (s < nh + LA))
            def _():
                b = s - LA + o * nh
                for k in range(2):
                    own(o, k, b).wait_recv()
                    fwd(o, k, b).start()

        @pl.when(s == 1)
        def _():
            load_wz.wait()
            for k in range(4):
                load_wx(k).wait()
            for k in range(3):
                wz(k).wait_recv()
                for j in range(4):
                    wx(k, j).wait_recv()
            for o in range(2):
                for k in range(3):
                    wy(o, k).start()
                wc(o, 0).start()

        @pl.when(s == 7)
        def _():
            for o in range(2):
                for k in range(3):
                    wy(o, k).wait_recv()
                    wc(o, k + 1).start()

        @pl.when(s >= nh)
        def _():
            for k in range(2):
                i = 2 * (s - nh) + k
                gw_tile(2 * lax.rem(i, 4) + jnp.where(i < 4, 1 - core, core))

        @pl.when((s >= nh) & (s < nh + 2))
        def _():
            for k in range(2):
                gx(2 * (s - nh) + k).start()

    for o in range(2):
        for k in range(4):
            wc(o, k).wait_recv()

    mh = nc // 2
    LD = 2
    LE = 4

    @pl.loop(0, mh + LE)
    def _(s):
        @pl.when(s < mh)
        def _():
            for o in range(2):
                for k in range(2):
                    fwd(o, k, s + o * nh).wait_recv()

            for o in range(2):
                c = s + o * mh
                lhs = jnp.concatenate([g[k, span(c * RB, RB), :] for k in range(4)], axis=1)
                part = jnp.dot(lhs, wq[o].reshape(1024, 1024), preferred_element_type=F32).astype(BF16)
                for k in range(4):
                    p[k, span(c * RB, RB), :] = part[:, k * 256:(k + 1) * 256]
                for k in range(2):
                    hop(o, k, c).start()
                for k in range(2):
                    direct(o, k, c).start()

        @pl.when((s >= LD) & (s < mh + LD))
        def _():
            for o in range(2):
                c = s - LD + o * mh
                right, left, _ = reduce_at[o]
                hop(o, 0, c).wait_recv()
                a1[c] = add(a1[c], p[right, half_a(c), :])
                two(o, 0, c).start()
                hop(o, 1, c).wait_recv()
                b1[c] = add(b1[c], p[left, half_b(c), :])
                two(o, 1, c).start()

        @pl.when(s >= LE)
        def _():
            for o in range(2):
                c = s - LE + o * mh
                me = reduce_me[o]
                direct(o, 1, c).wait_recv()
                two(o, 0, c).wait_recv()
                out[half_a(c), :] = add(p[me, half_a(c), :], a2[c], dr[c])
                direct(o, 0, c).wait_recv()
                two(o, 1, c).wait_recv()
                out[half_b(c), :] = add(p[me, half_b(c), :], b2[c], dl[c])

        @pl.when(s == 0)
        def _():
            for k in range(4):
                gx(k).wait_recv()
                gwx[k] = add(gwx[k], gwt[2 * k + core])
            for k in range(4):
                gy(k).start()

        @pl.when(s == 2)
        def _():
            gy(0).wait_recv()
            ga1[...] = add(ga1[...], gwx[ys[0], A, :])
            gy(4).start()
            gy(1).wait_recv()
            gb1[...] = add(gb1[...], gwx[ys[1], B, :])
            gy(5).start()

        @pl.when(s == 4)
        def _():
            gy(3).wait_recv()
            gy(4).wait_recv()
            gwo[A, :] = add(gwx[y, A, :], ga2[...], gdr[...])
            gy(2).wait_recv()
            gy(5).wait_recv()
            gwo[B, :] = add(gwx[y, B, :], gb2[...], gdl[...])

    for k in range(3):
        wz(k).wait_send()
        for j in range(4):
            wx(k, j).wait_send()
        for o in range(2):
            wy(o, k).wait_send()
    for k in range(4):
        gx(k).wait_send()
        for o in range(2):
            wc(o, k).wait_send()
    for k in range(6):
        gy(k).wait_send()

    @pl.loop(0, nh)
    def _(s):
        for o in range(2):
            for k in range(2):
                own(o, k, s + o * nh).wait_send()
                fwd(o, k, s + o * nh).wait_send()

    @pl.loop(0, mh)
    def _(s):
        for o in range(2):
            c = s + o * mh
            for k in range(2):
                hop(o, k, c).wait_send()
                direct(o, k, c).wait_send()
                two(o, k, c).wait_send()


def local(hidden, weight, block_ids, targets):
    rows, width = hidden.shape
    owned = weight.shape[0]
    nb, nc = rows // RL, rows // RB
    dma = pltpu.SemaphoreType.DMA
    v = lambda *shape: pltpu.VMEM(shape, BF16)
    scratch = [
        v(rows, width), v(owned, width), v(2, 4, owned, 1024), v(4, rows, owned), v(owned, rows), v(4, rows, 256),
    ] + [v(nc, RB // 2, 256)] * 6 + [
        v(8, owned, 512), v(4, owned, 512),
    ] + [v(128, 512)] * 6 + [
        dma((nb,)), dma((6,)),
        dma((3,)), dma((3,)), dma((3, 4)), dma((3, 4)), dma((2, 3)), dma((2, 3)), dma((2, 4)), dma((2, 4)),
    ] + [dma((2, nb))] * 4 + [dma((2, nc))] * 6 + [dma((4,)), dma((4,)), dma((6,)), dma((6,))]
    anywhere = pl.BlockSpec(memory_space=pl.ANY)
    return pl.pallas_call(
        kernel,
        out_shape=(pltpu.VMEM((rows, 256), BF16), pltpu.VMEM((owned, 512), BF16)),
        in_specs=[pl.BlockSpec(memory_space=pltpu.SMEM), pl.BlockSpec(memory_space=pltpu.VMEM), anywhere, anywhere],
        out_specs=(pl.BlockSpec(memory_space=pltpu.VMEM),) * 2,
        scratch_shapes=scratch,
        compiler_params=pltpu.CompilerParams(
            collective_id=0, has_side_effects=True, vmem_limit_bytes=57 * 1024 * 1024),
        cost_estimate=pl.CostEstimate(
            flops=6 * rows * owned * width, bytes_accessed=2 * rows * width, transcendentals=rows * owned),
    )(block_ids.T, targets.T, hidden, weight)


def solution(mesh):
    return jax.shard_map(
        local,
        mesh=mesh,
        in_specs=(P("dp", None), P("head", None), P("dp", None), P("dp", None)),
        out_specs=(P("dp", "head"), P("head", "dp")),
        check_vma=False,
    )
```

```python
import jax
import jax.numpy as jnp
from jax import lax
from jax.experimental import pallas as pl
from jax.experimental.pallas import tpu as pltpu
from jax.sharding import PartitionSpec as P

MESH = pl.DeviceIdType.MESH
BLOCK = 128
F32 = jnp.float32
BF16 = jnp.bfloat16
RL = 256
RB = 256


def kernel(ids_ref, tgt_ref, hid_hbm, w_hbm, out, gwo,
           hid, w, wq, g, gt, p, a1, b1, a2, b2, dl, dr,
           gwt, gwx, ga1, gb1, ga2, gb2, gdl, gdr,
           hid_sem, w_sem,
           wz_s, wz_r, wx_s, wx_r, wy_s, wy_r, wc_s, wc_r,
           own_s, own_r, fwd_s, fwd_r, hop_s, hop_r, dir_s, dir_r, two_s, two_r,
           gx_s, gx_r, gy_s, gy_r):
    rows = hid.shape[0]
    half = RB // 2
    nb = rows // RL
    nc = rows // RB
    dp = lax.axis_index("dp")
    head = lax.axis_index("head")
    y, core = dp // 2, dp % 2
    z, x = head // 4, head % 4

    def ring(v):
        return lax.rem(v + 1, 4), lax.rem(v + 3, 4), lax.rem(v + 2, 4)

    zs, xs, ys = ring(z), ring(x), ring(y)
    to_z = [(dp, v * 4 + x) for v in zs]
    to_x = [(dp, z * 4 + v) for v in xs]
    to_y = [(v * 2 + core, head) for v in ys]
    gather_to = (to_z, to_x)
    reduce_to = (to_x, to_z)
    reduce_at = (xs, zs)
    reduce_me = (x, z)
    sibling = (y * 2 + 1 - core, head)

    def remote(src, dst, ss, rs, dev):
        return pltpu.make_async_remote_copy(
            src_ref=src, dst_ref=dst, send_sem=ss, recv_sem=rs, device_id=dev, device_id_type=MESH)

    def span(start, size):
        return pl.ds(pl.multiple_of(start, size), size)

    def block(b):
        return span(b * RL, RL)

    def low(b):
        return span(b * RL, RL // 2)

    def high(b):
        return span(b * RL + RL // 2, RL // 2)

    def half_a(c):
        return span(c * RB, half)

    def half_b(c):
        return span(c * RB + half, half)

    def load_hid(b):
        return pltpu.make_async_copy(hid_hbm.at[block(b)], hid.at[block(b)], hid_sem.at[b])

    load_w = pltpu.make_async_copy(w_hbm, w, w_sem.at[0])
    load_wz = pltpu.make_async_copy(w_hbm.at[:, span(z * 1024, 1024)], wq.at[0, 0], w_sem.at[1])

    def load_wx(k):
        return pltpu.make_async_copy(
            w_hbm.at[:, span((k * 4 + x) * 256, 256)], wq.at[1, 0, :, pl.ds(k * 256, 256)], w_sem.at[2 + k])

    load_w.start()
    load_hid(0).start()
    load_hid(nb // 2).start()

    load_wz.start()
    for k in range(4):
        load_wx(k).start()

    barrier = pltpu.get_barrier_semaphore()
    peers = to_z + to_x + to_y + [sibling]
    for dev in peers:
        pl.semaphore_signal(barrier, inc=1, device_id=dev, device_id_type=MESH)
    pl.semaphore_wait(barrier, len(peers))

    piece = w.shape[0] // 8
    mine = span(dp * piece, piece)

    def wz(k):
        return remote(w_hbm.at[mine, span(zs[k] * 1024, 1024)], wq.at[0, k + 1, mine],
                      wz_s.at[k], wz_r.at[k], to_z[k])

    def wx(k, j):
        return remote(w_hbm.at[mine, span((j * 4 + xs[k]) * 256, 256)], wq.at[1, k + 1, mine, pl.ds(j * 256, 256)],
                      wx_s.at[k, j], wx_r.at[k, j], to_x[k])

    def wy(o, k):
        part = wq.at[o, pl.ds(1, 3), mine]
        return remote(part, part, wy_s.at[o, k], wy_r.at[o, k], to_y[k])

    def wc(o, k):
        frm = (y, ys[1], ys[0], ys[2])[k] * 2 + core
        part = wq.at[o, pl.ds(1, 3), span(frm * piece, piece)]
        return remote(part, part, wc_s.at[o, k], wc_r.at[o, k], sibling)

    for k in range(3):
        wz(k).start()
        for j in range(4):
            wx(k, j).start()

    def own(o, k, b):
        return remote(g.at[0, block(b)], g.at[k + 1, block(b)], own_s.at[k, b], own_r.at[k, b], gather_to[o][k])

    def fwd(o, k, b):
        part = (low, high)[k](b)
        return remote(g.at[k + 1, part], g.at[3, part], fwd_s.at[k, b], fwd_r.at[k, b], gather_to[o][k])

    def hop(o, k, c):
        part, dst = ((half_a(c), a1), (half_b(c), b1))[k]
        return remote(p.at[reduce_at[o][2], part], dst.at[c], hop_s.at[k, c], hop_r.at[k, c], reduce_to[o][k])

    def direct(o, k, c):
        part, dst = ((half_b(c), dl), (half_a(c), dr))[k]
        return remote(p.at[reduce_at[o][k], part], dst.at[c], dir_s.at[k, c], dir_r.at[k, c], reduce_to[o][k])

    def two(o, k, c):
        src, dst = ((a1, a2), (b1, b2))[k]
        return remote(src.at[c], dst.at[c], two_s.at[k, c], two_r.at[k, c], reduce_to[o][k])

    first = head * 2
    labels = first * BLOCK + lax.broadcasted_iota(jnp.int32, (2 * BLOCK, RL), 0)
    upper = lax.broadcasted_iota(jnp.int32, (2 * BLOCK, RL), 0) >= BLOCK

    def signal(b):
        load_hid(b).wait()
        t = lax.dot_general(w[...], hid[block(b), :], (((1,), (1,)), ((), ())), preferred_element_type=F32)
        lo = jnp.int32(0)
        hi = jnp.int32(0)
        for k in range(ids_ref.shape[0]):
            ident = ids_ref[k, b]
            lo = lo + (ident == first).astype(jnp.int32)
            hi = hi + (ident == first + 1).astype(jnp.int32)
        tg = tgt_ref[:, block(b)]
        hits = labels == tg[0:1, :]
        for k in range(1, tgt_ref.shape[0]):
            hits = hits | (labels == tg[k:k + 1, :])
        s = jax.nn.sigmoid(t) - hits.astype(F32)
        s = jnp.where(jnp.where(upper, hi, lo) > 0, s, 0.0)
        gt[:, block(b)] = s.astype(BF16)
        g[0, block(b), :] = s.T.astype(BF16)

    def gw_tile(j):
        t = jnp.dot(gt[...], hid[:, span(j * 512, 512)], preferred_element_type=F32)
        gwt[j] = t.astype(BF16)

    def gx(k):
        return remote(gwt.at[2 * k + 1 - core], gwx.at[k], gx_s.at[k], gx_r.at[k], sibling)

    A, B = pl.ds(0, 128), pl.ds(128, 128)

    def gy(k):
        src, dst, to = (
            (gwx.at[ys[2], A], ga1, 0), (gwx.at[ys[2], B], gb1, 1),
            (gwx.at[ys[0], B], gdl, 0), (gwx.at[ys[1], A], gdr, 1),
            (ga1, ga2, 0), (gb1, gb2, 1))[k]
        return remote(src, dst, gy_s.at[k], gy_r.at[k], to_y[to])

    def add(*parts):
        total = parts[0].astype(F32)
        for part in parts[1:]:
            total = total + part.astype(F32)
        return total.astype(BF16)

    load_w.wait()

    nh = nb // 2
    for o in range(2):
        load_hid(o * nh + 1).start()

    LA = 4

    @pl.loop(0, nh + LA)
    def _(s):
        for o in range(2):
            @pl.when(s < nh)
            def _():
                b = s + o * nh

                @pl.when(s < nh - 2)
                def _():
                    load_hid(b + 2).start()

                signal(b)
                for k in range(2):
                    own(o, k, b).start()

            @pl.when((s >= LA) & (s < nh + LA))
            def _():
                b = s - LA + o * nh
                for k in range(2):
                    own(o, k, b).wait_recv()
                    fwd(o, k, b).start()

        @pl.when(s == 1)
        def _():
            load_wz.wait()
            for k in range(4):
                load_wx(k).wait()
            for k in range(3):
                wz(k).wait_recv()
                for j in range(4):
                    wx(k, j).wait_recv()
            for o in range(2):
                for k in range(3):
                    wy(o, k).start()
                wc(o, 0).start()

        @pl.when(s == 8)
        def _():
            for o in range(2):
                for k in range(3):
                    wy(o, k).wait_recv()
                    wc(o, k + 1).start()

        @pl.when((s >= nh) & (s < nh + 2))
        def _():
            for k in range(2):
                gw_tile(2 * (2 * (s - nh) + k) + 1 - core)

        @pl.when((s >= nh) & (s < nh + 2))
        def _():
            for k in range(2):
                gx(2 * (s - nh) + k).start()

    for o in range(2):
        for k in range(4):
            wc(o, k).wait_recv()

    mh = nc // 2
    LD = 2
    LE = 4

    @pl.loop(0, mh + LE)
    def _(s):
        @pl.when(s < mh)
        def _():
            for o in range(2):
                for k in range(2):
                    fwd(o, k, s + o * nh).wait_recv()

            for o in range(2):
                c = s + o * mh
                lhs = jnp.concatenate([g[k, span(c * RB, RB), :] for k in range(4)], axis=1)
                part = jnp.dot(lhs, wq[o].reshape(1024, 1024), preferred_element_type=F32).astype(BF16)
                for k in range(4):
                    p[k, span(c * RB, RB), :] = part[:, k * 256:(k + 1) * 256]
                for k in range(2):
                    hop(o, k, c).start()
                for k in range(2):
                    direct(o, k, c).start()

        @pl.when(s < 4)
        def _():
            gw_tile(2 * s + core)

        @pl.when((s >= LD) & (s < mh + LD))
        def _():
            for o in range(2):
                c = s - LD + o * mh
                right, left, _ = reduce_at[o]
                hop(o, 0, c).wait_recv()
                a1[c] = add(a1[c], p[right, half_a(c), :])
                two(o, 0, c).start()
                hop(o, 1, c).wait_recv()
                b1[c] = add(b1[c], p[left, half_b(c), :])
                two(o, 1, c).start()

        @pl.when(s >= LE)
        def _():
            for o in range(2):
                c = s - LE + o * mh
                me = reduce_me[o]
                direct(o, 1, c).wait_recv()
                two(o, 0, c).wait_recv()
                out[half_a(c), :] = add(p[me, half_a(c), :], a2[c], dr[c])
                direct(o, 0, c).wait_recv()
                two(o, 1, c).wait_recv()
                out[half_b(c), :] = add(p[me, half_b(c), :], b2[c], dl[c])

        @pl.when(s == 4)
        def _():
            for k in range(4):
                gx(k).wait_recv()
                gwx[k] = add(gwx[k], gwt[2 * k + core])
            for k in range(4):
                gy(k).start()

        @pl.when(s == 6)
        def _():
            gy(0).wait_recv()
            ga1[...] = add(ga1[...], gwx[ys[0], A, :])
            gy(4).start()
            gy(1).wait_recv()
            gb1[...] = add(gb1[...], gwx[ys[1], B, :])
            gy(5).start()

        @pl.when(s == 8)
        def _():
            gy(3).wait_recv()
            gy(4).wait_recv()
            gwo[A, :] = add(gwx[y, A, :], ga2[...], gdr[...])
            gy(2).wait_recv()
            gy(5).wait_recv()
            gwo[B, :] = add(gwx[y, B, :], gb2[...], gdl[...])

    for k in range(3):
        wz(k).wait_send()
        for j in range(4):
            wx(k, j).wait_send()
        for o in range(2):
            wy(o, k).wait_send()
    for k in range(4):
        gx(k).wait_send()
        for o in range(2):
            wc(o, k).wait_send()
    for k in range(6):
        gy(k).wait_send()

    @pl.loop(0, nh)
    def _(s):
        for o in range(2):
            for k in range(2):
                own(o, k, s + o * nh).wait_send()
                fwd(o, k, s + o * nh).wait_send()

    @pl.loop(0, mh)
    def _(s):
        for o in range(2):
            c = s + o * mh
            for k in range(2):
                hop(o, k, c).wait_send()
                direct(o, k, c).wait_send()
                two(o, k, c).wait_send()


def local(hidden, weight, block_ids, targets):
    rows, width = hidden.shape
    owned = weight.shape[0]
    nb, nc = rows // RL, rows // RB
    dma = pltpu.SemaphoreType.DMA
    v = lambda *shape: pltpu.VMEM(shape, BF16)
    scratch = [
        v(rows, width), v(owned, width), v(2, 4, owned, 1024), v(4, rows, owned), v(owned, rows), v(4, rows, 256),
    ] + [v(nc, RB // 2, 256)] * 6 + [
        v(8, owned, 512), v(4, owned, 512),
    ] + [v(128, 512)] * 6 + [
        dma((nb,)), dma((6,)),
        dma((3,)), dma((3,)), dma((3, 4)), dma((3, 4)), dma((2, 3)), dma((2, 3)), dma((2, 4)), dma((2, 4)),
    ] + [dma((2, nb))] * 4 + [dma((2, nc))] * 6 + [dma((4,)), dma((4,)), dma((6,)), dma((6,))]
    anywhere = pl.BlockSpec(memory_space=pl.ANY)
    return pl.pallas_call(
        kernel,
        out_shape=(pltpu.VMEM((rows, 256), BF16), pltpu.VMEM((owned, 512), BF16)),
        in_specs=[pl.BlockSpec(memory_space=pltpu.SMEM), pl.BlockSpec(memory_space=pltpu.VMEM), anywhere, anywhere],
        out_specs=(pl.BlockSpec(memory_space=pltpu.VMEM),) * 2,
        scratch_shapes=scratch,
        compiler_params=pltpu.CompilerParams(
            collective_id=0, has_side_effects=True, vmem_limit_bytes=57 * 1024 * 1024),
        cost_estimate=pl.CostEstimate(
            flops=6 * rows * owned * width, bytes_accessed=2 * rows * width, transcendentals=rows * owned),
    )(block_ids.T, targets.T, hidden, weight)


def solution(mesh):
    return jax.shard_map(
        local,
        mesh=mesh,
        in_specs=(P("dp", None), P("head", None), P("dp", None), P("dp", None)),
        out_specs=(P("dp", "head"), P("head", "dp")),
        check_vma=False,
    )
```
